32 devices in a mesh: seq: 8 (over z, y), head: 4 (over x, core).
Axes of the slice: x: 2, y: 2, z: 4, core: 2. Of those that a mesh axis runs over, the one named last changes fastest.
Arguments:
- queries: bfloat16 [2048, 2048], P('seq', 'head'), may hold values from -6 to 6
- keys: bfloat16 [2048, 2048], P('seq', 'head'), may hold values from -40 to 40
- values: bfloat16 [2048, 2048], P('seq', 'head'), may hold values from -24 to 24
- ridges: float32 [16], P('head'), may hold values from 0.25 to 4
- out_weight: bfloat16 [2048, 2048], P('head'), may hold values from -0.125 to 0.125
Outputs:
- layer_out: bfloat16 [2048, 2048], P('seq', 'head')
The draws below stay inside these ranges and needn't reach their ends.
All inputs are finite; a program needn't handle non-finite values.
Results may differ from the reference program's by a relative error of at most 0.0049.
Values may be sent and summed in bfloat16 or wider, within the bound.
A program may use at most 128 MiB of HBM per device.

```python
import math
import jax
import jax.numpy as jnp
from jax import lax

D = 2048
HEADS = 16
HD = 128
SPAN = 128
ITERS = 2
TOKENS = 2048


def draw_keys(key, part):
    first, second = jax.random.split(key, 2)
    scales = jnp.exp(jax.random.uniform(first, (1, HEADS * HD), jnp.float32, 0.0, math.log(10.0)))
    base = jax.random.normal(second, (TOKENS, HEADS * HD), jnp.float32) * scales
    return jnp.clip(base, -40.0, 40.0).astype(jnp.bfloat16)


def levels(own_key, dims, pieces, smallest, largest):
    loudness, own = 1.0, jax.random.fold_in(own_key, 6)
    for axis_at, shards_of in pieces:
        steps = jnp.exp(jax.random.uniform(jax.random.fold_in(own, axis_at), (shards_of,), jnp.float32, smallest / len(pieces), largest / len(pieces)))
        loudness = loudness * jnp.repeat(steps, dims[axis_at] // shards_of).reshape([-1 if axis == axis_at else 1 for axis in range(len(dims))])
    return loudness


def noise(stream_key, dims, width, most, cuts=(), held_as=jnp.bfloat16):
    level = levels(stream_key, dims, cuts, -0.22, 0.18) if cuts else 1.0
    values = jax.random.normal(stream_key, dims, jnp.float32) * width * level
    return jnp.minimum(jnp.maximum(values, -most), most).astype(held_as)


def setup_inputs(seed: int = 0) -> dict:
    arg_keys = jax.random.split(jax.random.key(seed), 6)
    queries = noise(arg_keys[0], (TOKENS, HEADS * HD), 1.0, 6.0, ((0, 8), (1, 4)))
    keys = draw_keys(jax.random.fold_in(arg_keys[5], 71), 0)
    values = noise(arg_keys[2], (TOKENS, HEADS * HD), 4.0, 24.0, ((0, 8), (1, 4)))
    ridges = jnp.clip(jnp.exp(math.log(4.0) - 2.7725887 * jax.random.uniform(arg_keys[3], (HEADS,), jnp.float32) ** levels(arg_keys[3], (HEADS,), ((0, 4),), -0.2, 0.2)), 0.25, 4.0)
    out_weight = noise(arg_keys[4], (HEADS * HD, D), (HEADS * HD) ** -0.5, 0.125, ((0, 4),))
    return dict(queries=queries, keys=keys, values=values, ridges=ridges, out_weight=out_weight)


highest = lax.Precision.HIGHEST

def normalize(entries):
    return entries * lax.rsqrt(lax.optimization_barrier(jnp.sum(entries * entries, axis=-1, keepdims=True)) + 1e-06)

def product(left, right):
    return jnp.dot(left, right, precision=highest, preferred_element_type=jnp.float32)

def solve_block(queries_b, keyrows, values_b, key_state, value_state, ridge_value):
    block_len = queries_b.shape[0]
    causal = (lax.broadcasted_iota(jnp.int32, (block_len, block_len), 0) >= lax.broadcasted_iota(jnp.int32, (block_len, block_len), 1)).astype(jnp.float32)

    def within(inputs, payload):
        scores = product(inputs, keyrows.T) * causal
        return product(scores, payload)

    def operate(direction):
        return ridge_value * direction + within(direction, keyrows) + product(direction, key_state)
    estimate = jnp.zeros_like(queries_b)
    residual = queries_b
    direction = queries_b
    res_norm = lax.optimization_barrier(jnp.sum(residual * residual, axis=-1, keepdims=True))
    for sweep in range(ITERS):
        applied = operate(direction)
        step_size = res_norm / (lax.optimization_barrier(jnp.sum(direction * applied, axis=-1, keepdims=True)) + 1e-06)
        estimate = estimate + step_size * direction
        residual = residual - step_size * applied
        fresh = lax.optimization_barrier(jnp.sum(residual * residual, axis=-1, keepdims=True))
        direction = residual + fresh / (res_norm + 1e-06) * direction
        res_norm = fresh
    return product(estimate, value_state) + within(estimate, values_b)

def one_head(operands):
    head_q, head_k, head_v, ridge_value = operands
    blocks_q = normalize(head_q).reshape(-1, SPAN, HD)
    blocks_k = normalize(head_k).reshape(-1, SPAN, HD)
    blocks_v = head_v.reshape(-1, SPAN, HD)

    def advance(carry, block):
        key_state, value_state = carry
        block_q, block_k, block_v = block
        result = solve_block(block_q, block_k, block_v, key_state, value_state, ridge_value)
        key_state = key_state + product(block_k.T, block_k)
        value_state = value_state + product(block_k.T, block_v)
        return ((key_state, value_state), result)
    start = (jnp.zeros((HD, HD), jnp.float32), jnp.zeros((HD, HD), jnp.float32))
    unused, results = lax.scan(advance, start, (blocks_q, blocks_k, blocks_v))
    return results.reshape(TOKENS, HD)

def reference(queries, keys, values, ridges, out_weight):
    split_q = queries.astype(jnp.float32).reshape(TOKENS, HEADS, HD).transpose(1, 0, 2)
    split_k = keys.astype(jnp.float32).reshape(TOKENS, HEADS, HD).transpose(1, 0, 2)
    split_v = values.astype(jnp.float32).reshape(TOKENS, HEADS, HD).transpose(1, 0, 2)
    outputs = lax.map(one_head, (split_q, split_k, split_v, ridges.astype(jnp.float32)))
    mixed = outputs.transpose(1, 0, 2).reshape(TOKENS, HEADS * HD).astype(jnp.bfloat16)
    return jnp.dot(mixed, out_weight, preferred_element_type=jnp.float32).astype(jnp.bfloat16)
```

```python
import functools

import jax
import jax.numpy as jnp
from jax import lax
from jax.experimental import pallas as pl
from jax.experimental.pallas import tpu as pltpu
from jax.sharding import PartitionSpec as P

MESH = pl.DeviceIdType.MESH
EPS = 1e-06


def split(value):
    high = value.astype(jnp.bfloat16)
    return high, (value - high.astype(jnp.float32)).astype(jnp.bfloat16)


def product(left, right, dims=((1,), (0,))):
    return lax.dot_general(left, right, (dims, ((), ())), preferred_element_type=jnp.float32)


def row_sum(value):
    return jnp.sum(value, axis=-1, keepdims=True)


def kernel(
    seqs, groups, heads,
    q_any, k_any, v_any, ridge_ref, w_any, out_ref,
    q_ref, k_ref, v_ref, w_own, w_other,
    high_ref, low_ref, sums, sums_out, sums_in, run_out, run_in,
    qn_ref, first, mixed, mixed_in, part_out, part_in,
    load_sem, w_sem, ws_sem, wr_sem, ss_sem, sr_sem, rs_sem, rr_sem, ms_sem, mr_sem, ps_sem, pr_sem,
):
    seq, group = lax.axis_index("seq"), lax.axis_index("head")
    rank, side = seq // 2, seq % 2
    pair, lane = group // 2, group % 2
    ranks, pairs = seqs // 2, groups // 2
    tokens, width = out_ref.shape
    hd = q_ref.shape[1] // heads
    twin_seq, twin_head = seq + 1 - 2 * side, group + 1 - 2 * lane
    not_first, not_last = rank > 0, rank < ranks - 1

    loads = [
        pltpu.make_async_copy(src, dst, load_sem.at[at])
        for at, (src, dst) in enumerate(((k_any, k_ref), (v_any, v_ref), (q_any, q_ref)))
    ]
    for load in loads:
        load.start()

    def columns(at, parity):
        return pl.ds(pl.multiple_of((2 * at + parity) * width, 128), width)

    w_loads = [
        pltpu.make_async_copy(w_any.at[:, columns(at, lane)], w_own.at[at], w_sem.at[at])
        for at in range(pairs)
    ]
    for load in w_loads:
        load.start()

    barrier = pltpu.get_barrier_semaphore()

    def greet(**device):
        pl.semaphore_signal(barrier, inc=1, device_id=device, device_id_type=MESH)

    greet(seq=twin_seq)
    greet(head=twin_head)
    for off in range(1, pairs):
        greet(head=2 * ((pair + off) % pairs) + lane)

    @pl.when(not_first)
    def _():
        greet(seq=seq - 2)

    @pl.when(not_last)
    def _():
        greet(seq=seq + 2)

    pl.semaphore_wait(
        barrier, pairs + 1 + not_first.astype(jnp.int32) + not_last.astype(jnp.int32)
    )

    w_sends = [
        pltpu.make_async_remote_copy(
            w_any.at[:, columns(at, 1 - lane)], w_other.at[at], ws_sem.at[at], wr_sem.at[at],
            device_id={"head": twin_head}, device_id_type=MESH,
        )
        for at in range(pairs)
    ]

    loads[0].wait()
    loads[1].wait()
    sum_sends = []
    for at in range(heads):
        span = slice(at * hd, (at + 1) * hd)
        keys = k_ref[:, span].astype(jnp.float32)
        scale = lax.rsqrt(row_sum(keys * keys) + EPS)
        payload = jnp.concatenate(
            [keys * (scale * scale), v_ref[:, span].astype(jnp.float32) * scale], axis=1
        )
        high, low = split(payload)
        high_ref[at] = high
        low_ref[at] = low
        both = ((0,), (0,))
        total = product(k_ref[:, span], high, both) + product(k_ref[:, span], low, both)
        sums[at] = total
        sums_out[at] = total.astype(jnp.bfloat16)
        send = pltpu.make_async_remote_copy(
            sums_out.at[at], sums_in.at[at], ss_sem.at[at], sr_sem.at[at],
            device_id={"seq": twin_seq}, device_id_type=MESH,
        )
        send.start()
        sum_sends.append(send)

    for send in w_sends:
        send.start()

    causal = lax.broadcasted_iota(jnp.int32, (tokens, tokens), 0) >= lax.broadcasted_iota(
        jnp.int32, (tokens, tokens), 1
    )

    def within(at, parts):
        keys = k_ref[:, at * hd:(at + 1) * hd]
        across = ((1,), (1,))
        scores = product(parts[0], keys, across) + product(parts[1], keys, across)
        high, low = split(jnp.where(causal, scores, 0.0))
        payload = high_ref[at]
        return product(high, payload) + product(low, payload) + product(high, low_ref[at])

    loads[2].wait()
    for at in range(heads):
        q = q_ref[:, at * hd:(at + 1) * hd].astype(jnp.float32)
        q = q * lax.rsqrt(row_sum(q * q) + EPS)
        qn_ref[at] = q
        first[at] = within(at, split(q))

    mixed_sends = []
    run_sends = []
    for at in range(heads):
        run_sends.append(pltpu.make_async_remote_copy(
            run_out.at[at], run_in.at[at], rs_sem.at[at], rr_sem.at[at],
            device_id={"seq": (seq + 2) % seqs}, device_id_type=MESH,
        ))

        @pl.when(rank == 0)
        def _():
            run_in[at] = jnp.zeros(run_in.shape[1:], run_in.dtype)

        sum_sends[at].wait_recv()

        @pl.when(not_first)
        def _():
            run_sends[at].wait_recv()

        @pl.when(not_last)
        def _():
            run_out[at] = (
                run_in[at].astype(jnp.float32) + (sums[at] + sums_in[at].astype(jnp.float32))
            ).astype(jnp.bfloat16)
            run_sends[at].start()

        near = jnp.where(side == 1, sums_in[at], jnp.zeros(sums_in.shape[1:], jnp.bfloat16))
        state = jnp.concatenate([run_in[at], near], axis=0)

        def carried(parts):
            high, low = parts
            return product(jnp.concatenate([high, high], axis=1), state) + product(
                jnp.concatenate([low, low], axis=1), state
            )

        ridge = ridge_ref[at]
        q = qn_ref[at]
        whole = first[at] + carried(split(q))
        norm = row_sum(q * q)
        applied = whole[:, :hd] + ridge * q
        step = norm / (row_sum(q * applied) + EPS)
        residual = q - step * applied
        fresh = row_sum(residual * residual)
        direction = residual + fresh / (norm + EPS) * q
        parts = split(direction)
        again = within(at, parts) + carried(parts)
        applied = again[:, :hd] + ridge * direction
        after = fresh / (row_sum(direction * applied) + EPS)
        span = slice(at * hd, (at + 1) * hd)
        mixed[:, span] = (step * whole[:, hd:] + after * again[:, hd:]).astype(jnp.bfloat16)
        send = pltpu.make_async_remote_copy(
            mixed.at[:, span], mixed_in.at[:, span], ms_sem.at[at], mr_sem.at[at],
            device_id={"head": twin_head}, device_id_type=MESH,
        )
        send.start()
        mixed_sends.append(send)

    for load in w_loads:
        load.wait()
    for send in w_sends:
        send.wait_recv()
    for send in mixed_sends:
        send.wait_recv()

    def projected(index, rows):
        return product(mixed[rows, :], w_own[index]) + product(mixed_in[rows, :], w_other[index])

    cuts = part_out.shape[1]
    cut = tokens // cuts
    part_sends = []
    for off in range(1, pairs):
        target = (pair + off) % pairs
        for piece in range(cuts):
            part_out[off - 1, piece] = projected(
                target, slice(piece * cut, (piece + 1) * cut)
            ).astype(jnp.bfloat16)
            send = pltpu.make_async_remote_copy(
                part_out.at[off - 1, piece], part_in.at[off - 1, piece],
                ps_sem.at[off - 1, piece], pr_sem.at[off - 1, piece],
                device_id={"head": 2 * target + lane}, device_id_type=MESH,
            )
            send.start()
            part_sends.append(send)
    own = [projected(pair, slice(piece * cut, (piece + 1) * cut)) for piece in range(cuts)]
    for piece in range(cuts):
        total = own[piece]
        for off in range(1, pairs):
            part_sends[(off - 1) * cuts + piece].wait_recv()
            total = total + part_in[off - 1, piece].astype(jnp.float32)
        out_ref[piece * cut:(piece + 1) * cut, :] = total.astype(out_ref.dtype)

    for send in sum_sends + w_sends + mixed_sends + part_sends:
        send.wait_send()

    @pl.when(not_last)
    def _():
        for send in run_sends:
            send.wait_send()


def solution(mesh):
    seqs, groups = mesh.shape["seq"], mesh.shape["head"]

    def shards(queries, keys, values, ridges, out_weight):
        tokens, wide = queries.shape
        heads = ridges.shape[0]
        hd = wide // heads
        rows, model = out_weight.shape
        width = model // groups
        pairs = groups // 2
        cuts = 4
        bf16, f32 = jnp.bfloat16, jnp.float32
        dma = pltpu.SemaphoreType.DMA
        others = max(pairs - 1, 1)
        any_spec = pl.BlockSpec(memory_space=pl.ANY)
        return pl.pallas_call(
            functools.partial(kernel, seqs, groups, heads),
            out_shape=jax.ShapeDtypeStruct((tokens, width), bf16),
            in_specs=[any_spec, any_spec, any_spec, pl.BlockSpec(memory_space=pltpu.SMEM), any_spec],
            out_specs=pl.BlockSpec(memory_space=pltpu.VMEM),
            scratch_shapes=[
                pltpu.VMEM((tokens, wide), bf16),
                pltpu.VMEM((tokens, wide), bf16),
                pltpu.VMEM((tokens, wide), bf16),
                pltpu.VMEM((pairs, rows, width), bf16),
                pltpu.VMEM((pairs, rows, width), bf16),
                pltpu.VMEM((heads, tokens, 2 * hd), bf16),
                pltpu.VMEM((heads, tokens, 2 * hd), bf16),
                pltpu.VMEM((heads, hd, 2 * hd), f32),
                pltpu.VMEM((heads, hd, 2 * hd), bf16),
                pltpu.VMEM((heads, hd, 2 * hd), bf16),
                pltpu.VMEM((heads, hd, 2 * hd), bf16),
                pltpu.VMEM((heads, hd, 2 * hd), bf16),
                pltpu.VMEM((heads, tokens, hd), f32),
                pltpu.VMEM((heads, tokens, 2 * hd), f32),
                pltpu.VMEM((tokens, wide), bf16),
                pltpu.VMEM((tokens, wide), bf16),
                pltpu.VMEM((others, cuts, tokens // cuts, width), bf16),
                pltpu.VMEM((others, cuts, tokens // cuts, width), bf16),
                dma((3,)), dma((pairs,)), dma((pairs,)), dma((pairs,)),
                dma((heads,)), dma((heads,)), dma((heads,)), dma((heads,)),
                dma((heads,)), dma((heads,)), dma((others, cuts)), dma((others, cuts)),
            ],
            compiler_params=pltpu.CompilerParams(
                collective_id=0, has_side_effects=True, vmem_limit_bytes=48 * 2**20
            ),
        )(queries, keys, values, ridges, out_weight)

    in_specs = (P("seq", "head"), P("seq", "head"), P("seq", "head"), P("head"), P("head", None))
    return jax.shard_map(
        shards, mesh=mesh, in_specs=in_specs, out_specs=P("seq", "head"), check_vma=False
    )
```

```python
import functools

import jax
import jax.numpy as jnp
from jax import lax
from jax.experimental import pallas as pl
from jax.experimental.pallas import tpu as pltpu
from jax.sharding import PartitionSpec as P

MESH = pl.DeviceIdType.MESH
EPS = 1e-06


def split(value):
    high = value.astype(jnp.bfloat16)
    return high, (value - high.astype(jnp.float32)).astype(jnp.bfloat16)


def product(left, right, dims=((1,), (0,))):
    return lax.dot_general(left, right, (dims, ((), ())), preferred_element_type=jnp.float32)


def row_sum(value):
    return jnp.sum(value, axis=-1, keepdims=True)


def kernel(
    seqs, groups, heads,
    q_any, k_any, v_any, ridge_ref, w_any, out_ref,
    q_ref, k_ref, v_ref, w_own, w_other,
    high_ref, low_ref, sums, sums_out, sums_in, run_out, run_in, past_out, past_in,
    qn_ref, first, mixed, mixed_in, part_out, part_in,
    load_sem, w_sem, ws_sem, wr_sem, ss_sem, sr_sem, rs_sem, rr_sem, as_sem, ar_sem, ms_sem, mr_sem, ps_sem, pr_sem,
):
    seq, group = lax.axis_index("seq"), lax.axis_index("head")
    rank, side = seq // 2, seq % 2
    pair, lane = group // 2, group % 2
    ranks, pairs = seqs // 2, groups // 2
    tokens, width = out_ref.shape
    hd = q_ref.shape[1] // heads
    twin_seq, twin_head = seq + 1 - 2 * side, group + 1 - 2 * lane
    not_first, not_last = rank > 0, rank < ranks - 1

    loads = [
        pltpu.make_async_copy(src, dst, load_sem.at[at])
        for at, (src, dst) in enumerate(((k_any, k_ref), (v_any, v_ref), (q_any, q_ref)))
    ]
    for load in loads:
        load.start()

    def columns(at, parity):
        return pl.ds(pl.multiple_of((2 * at + parity) * width, 128), width)

    w_loads = [
        pltpu.make_async_copy(w_any.at[:, columns(at, lane)], w_own.at[at], w_sem.at[at])
        for at in range(pairs)
    ]
    for load in w_loads:
        load.start()

    barrier = pltpu.get_barrier_semaphore()

    def greet(**device):
        pl.semaphore_signal(barrier, inc=1, device_id=device, device_id_type=MESH)

    greet(seq=twin_seq)
    greet(head=twin_head)
    for off in range(1, pairs):
        greet(head=2 * ((pair + off) % pairs) + lane)

    @pl.when(not_first)
    def _():
        greet(seq=seq - 2)

    @pl.when(not_last)
    def _():
        greet(seq=seq + 2)

    w_sends = [
        pltpu.make_async_remote_copy(
            w_any.at[:, columns(at, 1 - lane)], w_other.at[at], ws_sem.at[at], wr_sem.at[at],
            device_id={"head": twin_head}, device_id_type=MESH,
        )
        for at in range(pairs)
    ]

    loads[0].wait()
    loads[1].wait()
    near, far = side, 1 - side
    sum_sends = []
    for at in range(heads):
        span = slice(at * hd, (at + 1) * hd)
        keys = k_ref[:, span].astype(jnp.float32)
        scale = lax.rsqrt(row_sum(keys * keys) + EPS)
        payload = jnp.concatenate(
            [keys * (scale * scale), v_ref[:, span].astype(jnp.float32) * scale], axis=1
        )
        high, low = split(payload)
        high_ref[at] = high
        low_ref[at] = low
        both = ((0,), (0,))
        total = product(k_ref[:, span], high, both) + product(k_ref[:, span], low, both)
        sums[0, at] = total[:, :hd]
        sums[1, at] = total[:, hd:]
        sums_out[at] = sums[far, at].astype(jnp.bfloat16)
        if at == 0:
            pl.semaphore_wait(
                barrier, pairs + 1 + not_first.astype(jnp.int32) + not_last.astype(jnp.int32)
            )
        send = pltpu.make_async_remote_copy(
            sums_out.at[at], sums_in.at[at], ss_sem.at[at], sr_sem.at[at],
            device_id={"seq": twin_seq}, device_id_type=MESH,
        )
        send.start()
        sum_sends.append(send)

    for send in w_sends:
        send.start()

    causal = lax.broadcasted_iota(jnp.int32, (tokens, tokens), 0) >= lax.broadcasted_iota(
        jnp.int32, (tokens, tokens), 1
    )

    def within(at, parts):
        keys = k_ref[:, at * hd:(at + 1) * hd]
        across = ((1,), (1,))
        scores = product(parts[0], keys, across) + product(parts[1], keys, across)
        high, low = split(jnp.where(causal, scores, 0.0))
        payload = high_ref[at]
        return product(high, payload) + product(low, payload) + product(high, low_ref[at])

    loads[2].wait()
    for at in range(heads):
        q = q_ref[:, at * hd:(at + 1) * hd].astype(jnp.float32)
        q = q * lax.rsqrt(row_sum(q * q) + EPS)
        qn_ref[at] = q
        first[at] = within(at, split(q))

    bits = run_out.shape[1]
    bit = hd // bits
    run_sends = [
        [
            pltpu.make_async_remote_copy(
                run_out.at[at, piece], run_in.at[at, piece],
                rs_sem.at[at, piece], rr_sem.at[at, piece],
                device_id={"seq": (seq + 2) % seqs}, device_id_type=MESH,
            )
            for piece in range(bits)
        ]
        for at in range(heads)
    ]
    past_sends = [
        [
            pltpu.make_async_remote_copy(
                past_out.at[at, piece], past_in.at[at, piece],
                as_sem.at[at, piece], ar_sem.at[at, piece],
                device_id={"seq": twin_seq}, device_id_type=MESH,
            )
            for piece in range(bits)
        ]
        for at in range(heads)
    ]

    @pl.when(rank == 0)
    def _():
        run_in[...] = jnp.zeros(run_in.shape, run_in.dtype)

    def advance(at):
        sum_sends[at].wait_recv()
        for piece in range(bits):
            span = slice(piece * bit, (piece + 1) * bit)

            @pl.when(not_first)
            def _():
                run_sends[at][piece].wait_recv()

            @pl.when(not_last)
            def _():
                run_out[at, piece] = run_in[at, piece] + (
                    sums[near, at, span] + sums_in[at, span].astype(jnp.float32)
                )
                run_sends[at][piece].start()

            mine = jnp.where(side == 0, sums[near, at, span], 0.0)
            past_out[at, piece] = (run_in[at, piece] + mine).astype(jnp.bfloat16)
            past_sends[at][piece].start()

    mixed_sends = []

    def solve(at):
        before = jnp.where(side == 1, sums_in[at].astype(jnp.float32), 0.0)
        held, rest = split(run_in[at].reshape(hd, hd) + before)
        for piece in range(bits):
            past_sends[at][piece].wait_recv()
        given = past_in[at].reshape(hd, hd)
        none = jnp.zeros((hd, hd), jnp.bfloat16)
        left = side == 0
        state = jnp.concatenate(
            [
                jnp.concatenate([jnp.where(left, held, given), jnp.where(left, given, held)], axis=1),
                jnp.concatenate([jnp.where(left, rest, none), jnp.where(left, none, rest)], axis=1),
            ],
            axis=0,
        )

        def carried(parts):
            high, low = parts
            return product(jnp.concatenate([high, high], axis=1), state) + product(
                jnp.concatenate([low, low], axis=1), state
            )

        ridge = ridge_ref[at]
        q = qn_ref[at]
        whole = first[at] + carried(split(q))
        norm = row_sum(q * q)
        applied = whole[:, :hd] + ridge * q
        step = norm / (row_sum(q * applied) + EPS)
        residual = q - step * applied
        fresh = row_sum(residual * residual)
        direction = residual + fresh / (norm + EPS) * q
        parts = split(direction)
        again = within(at, parts) + carried(parts)
        applied = again[:, :hd] + ridge * direction
        after = fresh / (row_sum(direction * applied) + EPS)
        span = slice(at * hd, (at + 1) * hd)
        mixed[:, span] = (step * whole[:, hd:] + after * again[:, hd:]).astype(jnp.bfloat16)
        send = pltpu.make_async_remote_copy(
            mixed.at[:, span], mixed_in.at[:, span], ms_sem.at[at], mr_sem.at[at],
            device_id={"head": twin_head}, device_id_type=MESH,
        )
        send.start()
        mixed_sends.append(send)

    advance(0)
    for at in range(1, heads):
        advance(at)
        solve(at - 1)
    solve(heads - 1)

    for load in w_loads:
        load.wait()
    for send in w_sends:
        send.wait_recv()
    for send in mixed_sends[:-1]:
        send.wait_recv()
    most = (heads - 1) * hd

    def begun(index, rows):
        return product(mixed[rows, :], w_own[index]) + product(
            mixed_in[rows, :most], w_other[index, :most, :]
        )

    def ended(index, rows):
        return product(mixed_in[rows, most:], w_other[index, most:, :])

    cuts = part_out.shape[1]
    cut = tokens // cuts
    part_sends = []
    pieces = [slice(piece * cut, (piece + 1) * cut) for piece in range(cuts)]
    order = [(pair + off) % pairs for off in range(1, pairs)]
    starts = [[begun(target, rows) for rows in pieces] for target in order]
    mixed_sends[-1].wait_recv()
    for off, target in enumerate(order):
        for piece, rows in enumerate(pieces):
            part_out[off, piece] = (starts[off][piece] + ended(target, rows)).astype(jnp.bfloat16)
            send = pltpu.make_async_remote_copy(
                part_out.at[off, piece], part_in.at[off, piece],
                ps_sem.at[off, piece], pr_sem.at[off, piece],
                device_id={"head": 2 * target + lane}, device_id_type=MESH,
            )
            send.start()
            part_sends.append(send)
    own = [begun(pair, rows) + ended(pair, rows) for rows in pieces]
    for piece, rows in enumerate(pieces):
        total = own[piece]
        for off in range(pairs - 1):
            part_sends[off * cuts + piece].wait_recv()
            total = total + part_in[off, piece].astype(jnp.float32)
        out_ref[rows, :] = total.astype(out_ref.dtype)

    for send in sum_sends + w_sends + mixed_sends + part_sends + sum(past_sends, []):
        send.wait_send()

    @pl.when(not_last)
    def _():
        for send in sum(run_sends, []):
            send.wait_send()


def solution(mesh):
    seqs, groups = mesh.shape["seq"], mesh.shape["head"]

    def shards(queries, keys, values, ridges, out_weight):
        tokens, wide = queries.shape
        heads = ridges.shape[0]
        hd = wide // heads
        rows, model = out_weight.shape
        width = model // groups
        pairs = groups // 2
        cuts, bits = 4, 2
        bf16, f32 = jnp.bfloat16, jnp.float32
        dma = pltpu.SemaphoreType.DMA
        others = max(pairs - 1, 1)
        any_spec = pl.BlockSpec(memory_space=pl.ANY)
        return pl.pallas_call(
            functools.partial(kernel, seqs, groups, heads),
            out_shape=jax.ShapeDtypeStruct((tokens, width), bf16),
            in_specs=[any_spec, any_spec, any_spec, pl.BlockSpec(memory_space=pltpu.SMEM), any_spec],
            out_specs=pl.BlockSpec(memory_space=pltpu.VMEM),
            scratch_shapes=[
                pltpu.VMEM((tokens, wide), bf16),
                pltpu.VMEM((tokens, wide), bf16),
                pltpu.VMEM((tokens, wide), bf16),
                pltpu.VMEM((pairs, rows, width), bf16),
                pltpu.VMEM((pairs, rows, width), bf16),
                pltpu.VMEM((heads, tokens, 2 * hd), bf16),
                pltpu.VMEM((heads, tokens, 2 * hd), bf16),
                pltpu.VMEM((2, heads, hd, hd), f32),
                pltpu.VMEM((heads, hd, hd), bf16),
                pltpu.VMEM((heads, hd, hd), bf16),
                pltpu.VMEM((heads, bits, hd // bits, hd), f32),
                pltpu.VMEM((heads, bits, hd // bits, hd), f32),
                pltpu.VMEM((heads, bits, hd // bits, hd), bf16),
                pltpu.VMEM((heads, bits, hd // bits, hd), bf16),
                pltpu.VMEM((heads, tokens, hd), f32),
                pltpu.VMEM((heads, tokens, 2 * hd), f32),
                pltpu.VMEM((tokens, wide), bf16),
                pltpu.VMEM((tokens, wide), bf16),
                pltpu.VMEM((others, cuts, tokens // cuts, width), bf16),
                pltpu.VMEM((others, cuts, tokens // cuts, width), bf16),
                dma((3,)), dma((pairs,)), dma((pairs,)), dma((pairs,)),
                dma((heads,)), dma((heads,)),
                dma((heads, bits)), dma((heads, bits)), dma((heads, bits)), dma((heads, bits)),
                dma((heads,)), dma((heads,)), dma((others, cuts)), dma((others, cuts)),
            ],
            compiler_params=pltpu.CompilerParams(
                collective_id=0, has_side_effects=True, vmem_limit_bytes=63 * 2**20
            ),
        )(queries, keys, values, ridges, out_weight)

    in_specs = (P("seq", "head"), P("seq", "head"), P("seq", "head"), P("head"), P("head", None))
    return jax.shard_map(
        shards, mesh=mesh, in_specs=in_specs, out_specs=P("seq", "head"), check_vma=False
    )
```
